256 devices in a mesh: dp: 8 (over y, z_hi), expert: 32 (over z_lo, x, core).
Axes of the slice: x: 4, y: 4, z: 8 (z_hi: 2, z_lo: 4; z = z_hi * 4 + z_lo), core: 2. Of those that a mesh axis runs over, the one named last changes fastest.
Arguments:
- activations: bfloat16 [32768, 4096], P(('dp', 'expert')), may hold values from -6 to 6
- cotangent: bfloat16 [32768, 4096], P(('dp', 'expert')), may hold values from -6 to 6
- expert_ids: int32 [32768, 1], P(('dp', 'expert')), may hold values from 0 to 127; in each aligned block of 128 rows (0 to 127, 128 to 255, ...) at most 2 rows name the same one
- gate_probs: float32 [32768, 1], P(('dp', 'expert')), may hold values from 0.2 to 1
- gate_up: bfloat16 [32, 2, 4096, 1536], P('expert', None, None, 'dp'), may hold values from -0.09375 to 0.09375
- down_proj: bfloat16 [32, 1536, 4096], P('expert', 'dp'), may hold values from -0.15625 to 0.15625
Outputs:
- input_grad: bfloat16 [32768, 4096], P(('dp', 'expert'))
- grad_gate_up: bfloat16 [32, 2, 4096, 1536], P('expert', None, None, 'dp')
- grad_down: bfloat16 [32, 1536, 4096], P('expert', 'dp')
The draws below stay inside these ranges and needn't reach their ends.
Inputs may be any that keep to these rules, and one draw needn't show every extreme that they name: `expert_ids`: expert e < 32 is held by index e of the expert axis. Among the 128 tokens of one device no expert is named more than 2 times, a bound that some block reaches.
All inputs are finite; a program needn't handle non-finite values.
Results may differ from the reference program's by a relative error of at most 0.0058.
Values may be sent and summed in bfloat16 or wider, within the bound.
A program may use at most 128 MiB of HBM per device.

```python
import math
import jax
import jax.numpy as jnp
import numpy as np
from jax import lax

D = 4096
F = 1536
EXPERTS_ALL = 128
TOPK = 1
TOK_DEV = 128
EXPERTS = 32
CAP = 2
TOKENS = 32768
N_DP = 8
N_EXPERT = 32


def block_scale(stream_key, dims, pieces, least, top_value):
    factor_of = 1.0
    for position, shards_of in pieces:
        draws = jax.random.uniform(jax.random.fold_in(jax.random.fold_in(stream_key, 6), position), (shards_of,), jnp.float32, least / len(pieces), top_value / len(pieces))
        factor_of = factor_of * jnp.repeat(jnp.exp(draws), dims[position] // shards_of).reshape((-1,) + (1,) * (len(dims) - 1 - position))
    return factor_of


def deal_out(rng, own, number, rows, amount, top, reach, slope):
    ranking = jax.random.permutation(rng, amount)
    crowded, usual = shares(amount, rows * top, reach, slope, True), shares(amount, rows * top, reach, slope, False)
    places = jnp.arange(amount)

    def named(sizes, turn):
        used = int((sizes > 0).sum())
        fixed = max(1, used // 4)
        moved = fixed + (places - fixed + turn * (used - fixed)) % max(1, amount - fixed)
        return jnp.zeros((amount,), jnp.int32).at[ranking[jnp.where(places < fixed, places, moved)]].set(jnp.asarray(sizes, jnp.int32))

    sizes = jnp.where(number % 4 == 0, named(crowded, number // 4), named(usual, number - number // 4 - 1))
    mixed = jax.random.permutation(jax.random.fold_in(own, 3), amount)
    giver, taker = mixed[0:amount // 2 * 2:2], mixed[1:amount // 2 * 2:2]
    slack = jnp.minimum(sizes[giver] - 1, reach - sizes[taker]) // 2
    slack = jnp.where((giver == ranking[0]) | (taker == ranking[0]) | (sizes[taker] == 0), 0, jnp.maximum(slack, 0))
    moved = jax.random.randint(jax.random.fold_in(own, 4), (amount // 2,), 0, 1 << 20) % (slack + 1)
    sizes = sizes.at[giver].add(-moved).at[taker].add(moved)
    members = jnp.searchsorted(jnp.cumsum(sizes), jnp.arange(rows * top), side="right").astype(jnp.int32)
    table = members.reshape(top, rows).T
    table = table[jax.random.permutation(jax.random.fold_in(own, 1), rows)]
    turn = jax.random.randint(jax.random.fold_in(own, 2), (rows, 1), 0, top)
    return jnp.take_along_axis(table, (jnp.arange(top)[None, :] + turn) % top, axis=1)


def shares(number_of, total, limit, slope, full):
    loads = [(1 << 20) // math.isqrt(grade ** slope) + 1 for grade in range(1, number_of + 1)]
    largest = limit if full else min(limit, max(-(-total // number_of), total * loads[0] // sum(loads)))
    least = 1 if total - largest >= number_of - 1 else 0
    counts, surplus = [largest] + [least] * (number_of - 1), total - largest - least * (number_of - 1)
    while surplus > 0:
        candidates = [i for i in range(1, number_of) if counts[i] < largest] or [i for i in range(1, number_of) if counts[i] < limit]
        whole, left = sum([loads[i] for i in candidates]), surplus
        for i in candidates:
            extra = min(limit - counts[i], max(1, left * loads[i] // whole), surplus)
            counts[i] = counts[i] + extra
            surplus = surplus - extra
    return np.array(counts)


def bell_draw(key, dims, scale, bound, shards=(), held_as=jnp.bfloat16):
    array = jax.random.normal(key, dims, jnp.float32) * scale
    if len(shards) > 0:
        array = block_scale(key, dims, shards, -0.22, 0.18) * array
    return jnp.clip(array, min=-bound, max=bound).astype(held_as)


def setup_inputs(seed: int = 0) -> dict:
    key_of = jax.random.split(jax.random.key(seed), 7)
    activations = bell_draw(key_of[0], (TOKENS, D), 1.0, 6.0, ((0, 256),))
    cotangent = bell_draw(key_of[1], (TOKENS, D), 1.0, 6.0, ((0, 256),))
    expert_ids_keys = jax.random.split(jax.random.fold_in(key_of[2], 1), TOKENS // TOK_DEV)
    expert_ids_turns = jax.random.permutation(jax.random.fold_in(key_of[2], 3), TOKENS // TOK_DEV)
    expert_ids = jax.vmap(lambda own, number: deal_out(jax.random.fold_in(key_of[2], 2), own, number, TOK_DEV, EXPERTS_ALL, TOPK, CAP, 2))(expert_ids_keys, expert_ids_turns).reshape((TOKENS, TOPK))
    gate_probs = jnp.clip(0.2 + 0.8 * jax.random.uniform(key_of[3], (TOKENS, TOPK), jnp.float32) ** block_scale(key_of[3], (TOKENS, TOPK), ((0, 256),), -0.2, 0.2), 0.2, 1.0)
    gate_up = bell_draw(key_of[4], (EXPERTS, 2, D, F), D ** -0.5, 0.09375, ((0, 32), (3, 8)))
    down_proj = bell_draw(key_of[5], (EXPERTS, F, D), F ** -0.5, 0.15625, ((0, 32), (1, 8)))
    return {"activations": activations, "cotangent": cotangent, "expert_ids": expert_ids, "gate_probs": gate_probs, "gate_up": gate_up, "down_proj": down_proj}


def expert_backward(rows_tok, rows_cot, pair_weights, down_weights):
    pre_gate = jnp.dot(rows_tok, pair_weights[0], preferred_element_type=jnp.float32)
    pre_up = jnp.dot(rows_tok, pair_weights[1], preferred_element_type=jnp.float32)
    sigmoid_gate = jax.nn.sigmoid(pre_gate)
    activated = pre_gate * sigmoid_gate
    hidden = (activated * pre_up).astype(jnp.bfloat16)
    hidden_grad = jnp.dot(rows_cot, down_weights.T, preferred_element_type=jnp.float32)
    gate_grad = (hidden_grad * pre_up * sigmoid_gate * (1.0 + pre_gate * (1.0 - sigmoid_gate))).astype(jnp.bfloat16)
    up_grad = (hidden_grad * activated).astype(jnp.bfloat16)
    total_down = jnp.dot(hidden.T, rows_cot, preferred_element_type=jnp.float32)
    total_gate = jnp.dot(rows_tok.T, gate_grad, preferred_element_type=jnp.float32)
    total_up = jnp.dot(rows_tok.T, up_grad, preferred_element_type=jnp.float32)
    input_rows = jnp.dot(gate_grad, pair_weights[0].T, preferred_element_type=jnp.float32)
    input_rows = input_rows + jnp.dot(up_grad, pair_weights[1].T, preferred_element_type=jnp.float32)
    grads_pair = jnp.stack([total_gate, total_up]).astype(jnp.bfloat16)
    return input_rows.astype(jnp.bfloat16), grads_pair, total_down.astype(jnp.bfloat16)


def reference(activations, cotangent, expert_ids, gate_probs, gate_up, down_proj):
    identity = expert_ids[:, 0].astype(jnp.int32)
    rows_most = N_DP * N_EXPERT * CAP
    scaled = (gate_probs * cotangent.astype(jnp.float32)).astype(jnp.bfloat16)

    def one_expert(number):
        ordering = jnp.argsort((identity != number).astype(jnp.int32), stable=True)[:rows_most].astype(jnp.int32)
        chosen = identity[ordering] == number
        rows_tok = activations[ordering]
        rows_cot = jnp.where(chosen[:, None], scaled[ordering], jnp.zeros((), jnp.bfloat16))
        input_rows, grads_pair, grads_down = expert_backward(rows_tok, rows_cot, gate_up[number], down_proj[number])
        return ordering, input_rows, grads_pair, grads_down

    orderings, input_rows, grad_gate_up, grad_down = lax.map(one_expert, jnp.arange(EXPERTS, dtype=jnp.int32))
    input_grad = jnp.zeros((TOKENS, D), jnp.bfloat16).at[orderings.reshape(-1)].add(input_rows.reshape(-1, D))
    return input_grad, grad_gate_up, grad_down
```

```python
import jax
import jax.numpy as jnp
from jax import lax
from jax.experimental import pallas as pl
from jax.experimental.pallas import tpu as pltpu
from jax.sharding import PartitionSpec as P

CAP = 2
MESH = pl.DeviceIdType.MESH
F32 = jnp.float32
BF16 = jnp.bfloat16

NY = 4
NZH = 2
NZL = 4
NZ = NZH * NZL
NXC = 8
SLAB = NXC * CAP
OFFSETS = (0, 1, 7, 2, 6, 3, 5, 4)
CHUNK = 512


def nt(left, right):
    return lax.dot_general(left, right, (((1,), (1,)), ((), ())), preferred_element_type=F32)


def nn(left, right):
    return lax.dot_general(left, right, (((1,), (0,)), ((), ())), preferred_element_type=F32)


def tn(left, right):
    return lax.dot_general(left, right, (((0,), (0,)), ((), ())), preferred_element_type=F32)


def kernel(
    ids_ref,
    probs_ref,
    act_hbm,
    cot_hbm,
    pair_hbm,
    down_hbm,
    out_hbm,
    gpair_hbm,
    gdown_hbm,
    act,
    cot,
    pair,
    down,
    send,
    recv1,
    perm,
    rows,
    accs,
    gate_t,
    up_t,
    hid_t,
    own,
    part,
    relayed,
    from_up,
    from_down,
    summed,
    back,
    xsend,
    final,
    outv,
    gpair,
    gdown,
    load_sem,
    store_sem,
    x_send,
    x_recv,
    z_send,
    z_recv,
    y_send,
    y_recv,
    f_send,
    f_recv,
    rl_send,
    rl_recv,
    ru_send,
    ru_recv,
    rd_send,
    rd_recv,
    rz_send,
    rz_recv,
    rx_send,
    rx_recv,
):
    width = act.shape[1]
    chunks = width // CHUNK
    tokens = act.shape[0]
    e = lax.axis_index("expert")
    d = lax.axis_index("dp")
    zl = lax.div(e, NXC)
    xc = lax.rem(e, NXC)
    y = lax.div(d, NZH)
    z = lax.rem(d, NZH) * NZL + zl

    def dev(yy, zz, xx):
        return (yy * NZH + lax.div(zz, NZL), lax.rem(zz, NZL) * NXC + xx)

    def at_x(i):
        return dev(y, z, lax.rem(xc + i, NXC))

    def at_z(i):
        return dev(y, lax.rem(z + i, NZ), xc)

    up = dev(lax.rem(y + 1, NY), z, xc)
    dn = dev(lax.rem(y + NY - 1, NY), z, xc)

    def cols(c):
        return pl.ds(pl.multiple_of(c * CHUNK, CHUNK), CHUNK)

    def remote(src, dst, ssem, rsem, where):
        return pltpu.make_async_remote_copy(
            src_ref=src, dst_ref=dst, send_sem=ssem, recv_sem=rsem, device_id=where, device_id_type=MESH
        )

    loads = [
        pltpu.make_async_copy(act_hbm, act, load_sem.at[0]),
        pltpu.make_async_copy(cot_hbm, cot, load_sem.at[1]),
        pltpu.make_async_copy(pair_hbm, pair, load_sem.at[2]),
        pltpu.make_async_copy(down_hbm, down, load_sem.at[3]),
    ]
    for copy in loads:
        copy.start()
    barrier = pltpu.get_barrier_semaphore()
    partners = [at_x(i) for i in range(1, NXC)] + [at_z(i) for i in range(1, NZ)] + [up, dn]
    for partner in partners:
        pl.semaphore_signal(barrier, inc=1, device_id=partner, device_id_type=MESH)

    ids = ids_ref[...]
    ids_wide = jnp.broadcast_to(ids.astype(F32), (tokens, tokens))
    ids_tall = ids_wide.T
    row_at = lax.broadcasted_iota(jnp.int32, (tokens, tokens), 0)
    col_at = lax.broadcasted_iota(jnp.int32, (tokens, tokens), 1)
    earlier = jnp.where((ids_wide == ids_tall) & (row_at < col_at), 1.0, 0.0)
    rank = jnp.sum(earlier, axis=0, keepdims=True).astype(jnp.int32)
    offset = lax.rem(lax.div(ids, NXC) + NZL - zl, NZL)
    inside = ids < NZL * NXC
    place = lax.rem(ids, NXC) * (2 * NZL * CAP) + offset * CAP + rank
    place = jnp.where(inside, place, -1024)
    pick_tok = jnp.where(row_at == place, 1.0, 0.0).astype(BF16)
    pick_cot = jnp.where(row_at == place + NZL * CAP, 1.0, 0.0).astype(BF16)
    slot = lax.rem(ids, NXC) * (NZL * CAP) + offset * CAP + rank
    slot = jnp.where(inside, slot, -1024)
    half_row = lax.broadcasted_iota(jnp.int32, (NXC * NZL * CAP, tokens), 0)
    pick_out = jnp.where(half_row == slot, 1.0, 0.0).astype(BF16)

    loads[0].wait()
    loads[1].wait()
    probs = probs_ref[...]

    def gather_rows(c, carry):
        scaled = (probs * cot[:, cols(c)].astype(F32)).astype(BF16)
        got = nn(pick_tok, act[:, cols(c)]) + nn(pick_cot, scaled)
        got = got.astype(BF16).reshape(NXC, 2 * NZL * CAP, CHUNK)
        send[:, :, cols(c)] = got
        return carry

    lax.fori_loop(0, chunks, gather_rows, 0)
    pl.semaphore_wait(barrier, len(partners))

    x_copies = []
    for i in range(1, NXC):
        copy = remote(
            send.at[lax.rem(xc + i, NXC)], recv1.at[i], x_send.at[i], x_recv.at[i], at_x(i)
        )
        copy.start()
        x_copies.append(copy)
    own_copy = pltpu.make_async_copy(send.at[xc], recv1.at[0], load_sem.at[4])
    own_copy.start()
    for copy in x_copies:
        copy.wait_recv()
    own_copy.wait()

    prow = lax.broadcasted_iota(jnp.int32, (2 * NXC * NZL * CAP, 2 * NXC * NZL * CAP), 0)
    pcol = lax.broadcasted_iota(jnp.int32, (2 * NXC * NZL * CAP, 2 * NXC * NZL * CAP), 1)
    p_off = lax.div(prow, 2 * SLAB)
    p_kind = lax.rem(lax.div(prow, SLAB), 2)
    p_src = lax.rem(lax.div(prow, CAP), NXC)
    p_rank = lax.rem(prow, CAP)
    wanted = p_src * (2 * NZL * CAP) + p_kind * (NZL * CAP) + p_off * CAP + p_rank
    shuffle = jnp.where(pcol == wanted, 1.0, 0.0).astype(BF16)

    def shuffle_rows(c, carry):
        got = recv1[:, :, cols(c)].reshape(2 * NXC * NZL * CAP, CHUNK)
        moved = nn(shuffle, got).astype(BF16).reshape(NZL, 2, SLAB, CHUNK)
        perm[:, :, :, cols(c)] = moved
        rows[0, :, 0, :, cols(c)] = moved[0]
        return carry

    lax.fori_loop(0, chunks, shuffle_rows, 0)

    z_copies = [None]
    for k in range(1, NZ):
        copy = remote(
            perm.at[OFFSETS[k] % NZL], rows.at[k, :, 0], z_send.at[k], z_recv.at[k], at_z(OFFSETS[k])
        )
        copy.start()
        z_copies.append(copy)

    y_copies = {}
    f_copies = {}

    def forward(k):
        if k:
            z_copies[k].wait_recv()
        for way, (where, there) in enumerate(((up, 3), (dn, 1))):
            copy = remote(
                rows.at[k, :, 0], rows.at[k, :, there], y_send.at[way, k], y_recv.at[way, k], where
            )
            copy.start()
            y_copies[way, k] = copy

    def relay(k):
        way = k % 2
        y_copies[way, k].wait_recv()
        mine, where = ((3, up), (1, dn))[way]
        copy = remote(rows.at[k, :, mine], rows.at[k, :, 2], f_send.at[k], f_recv.at[k], where)
        copy.start()
        f_copies[k] = copy

    def arrived(g):
        for k in (2 * g, 2 * g + 1):
            y_copies[1 - k % 2, k].wait_recv()
            f_copies[k].wait_recv()

    group = 2 * NY * SLAB

    def compute(g):
        accs[...] = jnp.zeros_like(accs)

        def ahead(c, carry):
            tok = rows[2 * g : 2 * g + 2, 0, :, :, cols(c)].reshape(group, CHUNK)
            cts = rows[2 * g : 2 * g + 2, 1, :, :, cols(c)].reshape(group, CHUNK)
            accs[0] += nt(tok, pair[0, :, cols(c)])
            accs[1] += nt(tok, pair[1, :, cols(c)])
            accs[2] += nt(cts, down[:, cols(c)])
            return carry

        lax.fori_loop(0, chunks, ahead, 0)
        pre_gate, pre_up, hidden_grad = accs[0], accs[1], accs[2]
        sig = jax.nn.sigmoid(pre_gate)
        activated = pre_gate * sig
        hidden = (activated * pre_up).astype(BF16)
        gate_grad = (hidden_grad * pre_up * sig * (1.0 + pre_gate * (1.0 - sig))).astype(BF16)
        up_grad = (hidden_grad * activated).astype(BF16)
        span = slice(g * group, (g + 1) * group)
        gate_t[span, :] = gate_grad
        up_t[span, :] = up_grad
        hid_t[span, :] = hidden

        def behind(c, carry):
            got = nn(gate_grad, pair[0, :, cols(c)]) + nn(up_grad, pair[1, :, cols(c)])
            got = got.reshape(2, NY, SLAB, CHUNK)
            own[2 * g : 2 * g + 2, :, cols(c)] = got[:, 0]
            part[2 * g : 2 * g + 2, :, :, cols(c)] = got[:, 1:].astype(BF16)
            return carry

        lax.fori_loop(0, chunks, behind, 0)

    rl_copies = {}
    ru_copies = {}
    rd_copies = {}

    def give(k):
        if k % 2 == 0:
            rl = remote(part.at[k, 1], relayed.at[k], rl_send.at[k], rl_recv.at[k], up)
            direct = remote(part.at[k, 2], from_up.at[k], ru_send.at[k], ru_recv.at[k], dn)
            ru_copies[k] = direct
        else:
            rl = remote(part.at[k, 1], relayed.at[k], rl_send.at[k], rl_recv.at[k], dn)
            direct = remote(part.at[k, 0], from_down.at[k], rd_send.at[k], rd_recv.at[k], up)
            rd_copies[k] = direct
        rl.start()
        direct.start()
        rl_copies[k] = rl

    def give_on(k):
        rl_copies[k].wait_recv()
        mine = 0 if k % 2 == 0 else 2

        def add(c, carry):
            total = part[k, mine, :, cols(c)].astype(F32) + relayed[k, :, cols(c)].astype(F32)
            part[k, mine, :, cols(c)] = total.astype(BF16)
            return carry

        lax.fori_loop(0, chunks, add, 0)
        if k % 2 == 0:
            copy = remote(part.at[k, 0], from_down.at[k], rd_send.at[k], rd_recv.at[k], up)
            rd_copies[k] = copy
        else:
            copy = remote(part.at[k, 2], from_up.at[k], ru_send.at[k], ru_recv.at[k], dn)
            ru_copies[k] = copy
        copy.start()

    rz_copies = {}

    def settle(k):
        ru_copies[k].wait_recv()
        rd_copies[k].wait_recv()
        target = back if k == 0 else summed

        def add(c, carry):
            total = own[k, :, cols(c)] + (
                from_up[k, :, cols(c)].astype(F32) + from_down[k, :, cols(c)].astype(F32)
            )
            target[k, :, cols(c)] = total.astype(BF16)
            return carry

        lax.fori_loop(0, chunks, add, 0)
        if k:
            copy = remote(
                summed.at[k], back.at[k], rz_send.at[k], rz_recv.at[k], at_z(NZ - OFFSETS[k])
            )
            copy.start()
            rz_copies[k] = copy

    def weight_grads(which):
        def one(c, carry):
            kind = 0 if which < 2 else 1
            parts = [rows[2 * g : 2 * g + 2, kind, :, :, cols(c)].reshape(group, CHUNK) for g in range(4)]
            data = jnp.concatenate(parts, axis=0)
            got = tn((gate_t, up_t, hid_t)[which][...], data).astype(BF16)
            if which < 2:
                gpair[which, :, cols(c)] = got
            else:
                gdown[:, cols(c)] = got
            return carry

        lax.fori_loop(0, chunks, one, 0)
        if which < 2:
            copy = pltpu.make_async_copy(gpair.at[which], gpair_hbm.at[which], store_sem.at[which])
        else:
            copy = pltpu.make_async_copy(gdown, gdown_hbm, store_sem.at[which])
        copy.start()
        return copy

    forward(0)
    forward(1)
    forward(2)
    relay(0)
    relay(1)
    loads[2].wait()
    loads[3].wait()
    forward(3)
    relay(2)
    forward(4)
    relay(3)
    arrived(0)
    compute(0)
    give(0)
    give(1)
    forward(5)
    relay(4)
    forward(6)
    relay(5)
    arrived(1)
    compute(1)
    give(2)
    give(3)
    give_on(0)
    give_on(1)
    forward(7)
    relay(6)
    settle(0)
    settle(1)
    give_on(2)
    give_on(3)
    relay(7)
    arrived(2)
    compute(2)
    give(4)
    give(5)
    settle(2)
    settle(3)
    give_on(4)
    give_on(5)
    arrived(3)
    compute(3)
    give(6)
    give(7)
    settle(4)
    settle(5)
    stores = [weight_grads(0)]
    give_on(6)
    give_on(7)
    stores.append(weight_grads(1))
    settle(6)
    settle(7)
    stores.append(weight_grads(2))

    for k in range(1, NZ):
        rz_copies[k].wait_recv()
    half = NXC * NZL * CAP
    qrow = lax.broadcasted_iota(jnp.int32, (half, half), 0)
    qcol = lax.broadcasted_iota(jnp.int32, (half, half), 1)
    q_src = lax.div(qrow, NZL * CAP)
    q_off = lax.rem(lax.div(qrow, CAP), NZL)
    wanted_back = q_off * SLAB + q_src * CAP + lax.rem(qrow, CAP)
    shuffle_back = jnp.where(qcol == wanted_back, 1.0, 0.0).astype(BF16)

    def join(c, carry):
        parts = []
        for i in range(NZL):
            first, second = OFFSETS.index(i), OFFSETS.index(i + NZL)
            total = back[first, :, cols(c)].astype(F32) + back[second, :, cols(c)].astype(F32)
            parts.append(total.astype(BF16))
        moved = nn(shuffle_back, jnp.concatenate(parts, axis=0))
        for i in range(NXC):
            xsend[i, :, cols(c)] = moved[i * NZL * CAP : (i + 1) * NZL * CAP].astype(BF16)
        return carry

    lax.fori_loop(0, chunks, join, 0)

    rx_copies = []
    for i in range(1, NXC):
        copy = remote(
            xsend.at[i], final.at[xc], rx_send.at[i], rx_recv.at[i], at_x(NXC - i)
        )
        copy.start()
        rx_copies.append(copy)
    own_back = pltpu.make_async_copy(xsend.at[0], final.at[xc], load_sem.at[5])
    own_back.start()
    for copy in rx_copies:
        copy.wait_recv()
    own_back.wait()

    def place_out(c, carry):
        parts = [final[i, :, cols(c)].astype(F32) for i in range(NXC)]
        data = jnp.concatenate(parts, axis=0).astype(BF16)
        outv[:, cols(c)] = tn(pick_out, data).astype(BF16)
        return carry

    lax.fori_loop(0, chunks, place_out, 0)
    out_copy = pltpu.make_async_copy(outv, out_hbm, store_sem.at[3])
    out_copy.start()

    for copy in x_copies + z_copies[1:] + list(y_copies.values()) + list(f_copies.values()):
        copy.wait_send()
    for table in (rl_copies, ru_copies, rd_copies, rz_copies):
        for copy in table.values():
            copy.wait_send()
    for copy in rx_copies:
        copy.wait_send()
    for copy in stores:
        copy.wait()
    out_copy.wait()


def per_device(activations, cotangent, expert_ids, gate_probs, gate_up, down_proj):
    tokens, width = activations.shape
    units = down_proj.shape[1]
    pair = jnp.swapaxes(gate_up[0], 1, 2)
    down = down_proj[0]
    dma = pltpu.SemaphoreType.DMA
    vmem = pltpu.VMEM
    any_space = pl.BlockSpec(memory_space=pl.ANY)
    in_vmem = pl.BlockSpec(memory_space=pltpu.VMEM)
    total_rows = NZ * NY * SLAB
    out, gpair, gdown = pl.pallas_call(
        kernel,
        out_shape=(
            jax.ShapeDtypeStruct((tokens, width), BF16),
            jax.ShapeDtypeStruct((2, units, width), BF16),
            jax.ShapeDtypeStruct((units, width), BF16),
        ),
        in_specs=[in_vmem, in_vmem, any_space, any_space, any_space, any_space],
        out_specs=(any_space, any_space, any_space),
        scratch_shapes=[
            vmem((tokens, width), BF16),
            vmem((tokens, width), BF16),
            vmem((2, units, width), BF16),
            vmem((units, width), BF16),
            vmem((NXC, 2 * NZL * CAP, width), BF16),
            vmem((NXC, 2 * NZL * CAP, width), BF16),
            vmem((NZL, 2, SLAB, width), BF16),
            vmem((NZ, 2, NY, SLAB, width), BF16),
            vmem((3, 2 * NY * SLAB, units), F32),
            vmem((total_rows, units), BF16),
            vmem((total_rows, units), BF16),
            vmem((total_rows, units), BF16),
            vmem((NZ, SLAB, width), F32),
            vmem((NZ, NY - 1, SLAB, width), BF16),
            vmem((NZ, SLAB, width), BF16),
            vmem((NZ, SLAB, width), BF16),
            vmem((NZ, SLAB, width), BF16),
            vmem((NZ, SLAB, width), BF16),
            vmem((NZ, SLAB, width), BF16),
            vmem((NXC, NZL * CAP, width), BF16),
            vmem((NXC, NZL * CAP, width), BF16),
            vmem((tokens, width), BF16),
            vmem((2, units, width), BF16),
            vmem((units, width), BF16),
            dma((6,)),
            dma((4,)),
            dma((NXC,)),
            dma((NXC,)),
            dma((NZ,)),
            dma((NZ,)),
            dma((2, NZ)),
            dma((2, NZ)),
            dma((NZ,)),
            dma((NZ,)),
            dma((NZ,)),
            dma((NZ,)),
            dma((NZ,)),
            dma((NZ,)),
            dma((NZ,)),
            dma((NZ,)),
            dma((NZ,)),
            dma((NZ,)),
            dma((NXC,)),
            dma((NXC,)),
        ],
        compiler_params=pltpu.CompilerParams(
            collective_id=0, has_side_effects=True, vmem_limit_bytes=60 * 1024 * 1024
        ),
    )(expert_ids.reshape(1, tokens), gate_probs, activations, cotangent, pair, down)
    return out, jnp.swapaxes(gpair, 1, 2)[None], gdown[None]


def solution(mesh):
    in_specs = (
        P(("dp", "expert"), None),
        P(("dp", "expert"), None),
        P(("dp", "expert"), None),
        P(("dp", "expert"), None),
        P("expert", None, None, "dp"),
        P("expert", "dp", None),
    )
    out_specs = (P(("dp", "expert"), None), P("expert", None, None, "dp"), P("expert", "dp", None))
    return jax.shard_map(
        per_device, mesh=mesh, in_specs=in_specs, out_specs=out_specs, check_vma=False
    )
```

```python
import jax
import jax.numpy as jnp
from jax import lax
from jax.experimental import pallas as pl
from jax.experimental.pallas import tpu as pltpu
from jax.sharding import PartitionSpec as P

CAP = 2
MESH = pl.DeviceIdType.MESH
F32 = jnp.float32
BF16 = jnp.bfloat16

NY = 4
NZH = 2
NZL = 4
NZ = NZH * NZL
NXC = 8
SLAB = NXC * CAP
OFFSETS = (0, 1, 6, 2, 4, 5, 3, 7)
CHUNK = 512
HALVES = 2


def nt(left, right):
    return lax.dot_general(left, right, (((1,), (1,)), ((), ())), preferred_element_type=F32)


def nn(left, right):
    return lax.dot_general(left, right, (((1,), (0,)), ((), ())), preferred_element_type=F32)


def tn(left, right):
    return lax.dot_general(left, right, (((0,), (0,)), ((), ())), preferred_element_type=F32)


def kernel(
    ids_ref,
    probs_ref,
    act_hbm,
    cot_hbm,
    pair_hbm,
    down_hbm,
    pick_ref,
    final,
    gpair_hbm,
    gdown_hbm,
    act,
    cot,
    pair,
    down,
    send,
    recv1,
    perm,
    rows,
    accs,
    gate_t,
    up_t,
    hid_t,
    own,
    part,
    relayed,
    from_up,
    from_down,
    summed,
    back,
    xsend,
    gpair,
    gdown,
    load_sem,
    store_sem,
    x_send,
    x_recv,
    z_send,
    z_recv,
    y_send,
    y_recv,
    f_send,
    f_recv,
    rl_send,
    rl_recv,
    ru_send,
    ru_recv,
    rd_send,
    rd_recv,
    rz_send,
    rz_recv,
    rx_send,
    rx_recv,
):
    width = act.shape[1]
    chunks = width // CHUNK
    half_width = width // HALVES
    half_chunks = chunks // HALVES
    halves = range(HALVES)
    tokens = act.shape[0]
    e = lax.axis_index("expert")
    d = lax.axis_index("dp")
    zl = lax.div(e, NXC)
    xc = lax.rem(e, NXC)
    y = lax.div(d, NZH)
    z = lax.rem(d, NZH) * NZL + zl

    def dev(yy, zz, xx):
        return (yy * NZH + lax.div(zz, NZL), lax.rem(zz, NZL) * NXC + xx)

    def at_x(i):
        return dev(y, z, lax.rem(xc + i, NXC))

    def at_z(i):
        return dev(y, lax.rem(z + i, NZ), xc)

    up = dev(lax.rem(y + 1, NY), z, xc)
    dn = dev(lax.rem(y + NY - 1, NY), z, xc)

    def cols(c):
        return pl.ds(pl.multiple_of(c * CHUNK, CHUNK), CHUNK)

    def piece(h):
        return pl.ds(h * half_width, half_width)

    def over(h, body):
        lax.fori_loop(h * half_chunks, (h + 1) * half_chunks, body, 0)

    def remote(src, dst, ssem, rsem, where):
        return pltpu.make_async_remote_copy(
            src_ref=src, dst_ref=dst, send_sem=ssem, recv_sem=rsem, device_id=where, device_id_type=MESH
        )

    loads = [
        pltpu.make_async_copy(act_hbm, act, load_sem.at[0]),
        pltpu.make_async_copy(cot_hbm, cot, load_sem.at[1]),
        pltpu.make_async_copy(pair_hbm, pair, load_sem.at[2]),
        pltpu.make_async_copy(down_hbm, down, load_sem.at[3]),
    ]
    for copy in loads:
        copy.start()
    barrier = pltpu.get_barrier_semaphore()
    partners = [at_x(i) for i in range(1, NXC)] + [at_z(i) for i in range(1, NZ)] + [up, dn]
    for partner in partners:
        pl.semaphore_signal(barrier, inc=1, device_id=partner, device_id_type=MESH)

    ids = ids_ref[...]
    ids_wide = jnp.broadcast_to(ids.astype(F32), (tokens, tokens))
    ids_tall = ids_wide.T
    row_at = lax.broadcasted_iota(jnp.int32, (tokens, tokens), 0)
    col_at = lax.broadcasted_iota(jnp.int32, (tokens, tokens), 1)
    earlier = jnp.where((ids_wide == ids_tall) & (row_at < col_at), 1.0, 0.0)
    rank = jnp.sum(earlier, axis=0, keepdims=True).astype(jnp.int32)
    offset = lax.rem(lax.div(ids, NXC) + NZL - zl, NZL)
    inside = ids < NZL * NXC
    place = lax.rem(ids, NXC) * (2 * NZL * CAP) + offset * CAP + rank
    place = jnp.where(inside, place, -1024)
    pick_tok = jnp.where(row_at == place, 1.0, 0.0).astype(BF16)
    pick_cot = jnp.where(row_at == place + NZL * CAP, 1.0, 0.0).astype(BF16)
    slot = lax.rem(ids, NXC) * (NZL * CAP) + offset * CAP + rank
    slot = jnp.where(inside, slot, -1024)
    half_row = lax.broadcasted_iota(jnp.int32, (NXC * NZL * CAP, tokens), 0)
    pick_ref[...] = jnp.where(half_row == slot, 1.0, 0.0).astype(BF16)

    loads[0].wait()
    loads[1].wait()
    probs = jnp.broadcast_to(probs_ref[...], (tokens, tokens)).T[:, :1]

    def gather_rows(c, carry):
        scaled = (probs * cot[:, cols(c)].astype(F32)).astype(BF16)
        got = nn(pick_tok, act[:, cols(c)]) + nn(pick_cot, scaled)
        got = got.astype(BF16).reshape(NXC, 2 * NZL * CAP, CHUNK)
        send[:, :, cols(c)] = got
        return carry

    lax.fori_loop(0, chunks, gather_rows, 0)
    pl.semaphore_wait(barrier, len(partners))

    x_copies = {}
    for h in halves:
        for i in range(1, NXC):
            copy = remote(
                send.at[lax.rem(xc + i, NXC), :, piece(h)],
                recv1.at[i, :, piece(h)],
                x_send.at[h, i],
                x_recv.at[h, i],
                at_x(i),
            )
            copy.start()
            x_copies[h, i] = copy
    own_copy = pltpu.make_async_copy(send.at[xc], recv1.at[0], load_sem.at[4])
    own_copy.start()

    prow = lax.broadcasted_iota(jnp.int32, (2 * NXC * NZL * CAP, 2 * NXC * NZL * CAP), 0)
    pcol = lax.broadcasted_iota(jnp.int32, (2 * NXC * NZL * CAP, 2 * NXC * NZL * CAP), 1)
    p_off = lax.div(prow, 2 * SLAB)
    p_kind = lax.rem(lax.div(prow, SLAB), 2)
    p_src = lax.rem(lax.div(prow, CAP), NXC)
    p_rank = lax.rem(prow, CAP)
    wanted = p_src * (2 * NZL * CAP) + p_kind * (NZL * CAP) + p_off * CAP + p_rank
    shuffle = jnp.where(pcol == wanted, 1.0, 0.0).astype(BF16)

    def shuffle_rows(c, carry):
        got = recv1[:, :, cols(c)].reshape(2 * NXC * NZL * CAP, CHUNK)
        moved = nn(shuffle, got).astype(BF16).reshape(NZL, 2, SLAB, CHUNK)
        perm[:, :, :, cols(c)] = moved
        rows[0, :, 0, :, cols(c)] = moved[0]
        return carry

    def cross(h):
        for i in range(1, NXC):
            x_copies[h, i].wait_recv()
        over(h, shuffle_rows)

    z_copies = {}

    def spread(k, h):
        copy = remote(
            perm.at[OFFSETS[k] % NZL, :, :, piece(h)],
            rows.at[k, :, 0, :, piece(h)],
            z_send.at[h, k],
            z_recv.at[h, k],
            at_z(OFFSETS[k]),
        )
        copy.start()
        z_copies[k, h] = copy

    y_copies = {}
    f_copies = {}

    def forward(k, h):
        if k:
            z_copies[k, h].wait_recv()
        for way, (where, there) in enumerate(((up, 3), (dn, 1))):
            copy = remote(
                rows.at[k, :, 0, :, piece(h)],
                rows.at[k, :, there, :, piece(h)],
                y_send.at[way, h, k],
                y_recv.at[way, h, k],
                where,
            )
            copy.start()
            y_copies[way, k, h] = copy

    def relay(k, h):
        way = k % 2
        y_copies[way, k, h].wait_recv()
        mine, where = ((3, up), (1, dn))[way]
        copy = remote(
            rows.at[k, :, mine, :, piece(h)],
            rows.at[k, :, 2, :, piece(h)],
            f_send.at[h, k],
            f_recv.at[h, k],
            where,
        )
        copy.start()
        f_copies[k, h] = copy

    def arrived(k):
        for h in halves:
            y_copies[1 - k % 2, k, h].wait_recv()
            f_copies[k, h].wait_recv()

    per_slab = NY * SLAB

    def compute(k, count):
        group = count * per_slab
        accs[:, :group] = jnp.zeros((3, group, accs.shape[2]), F32)

        def ahead(c, carry):
            tok = rows[k : k + count, 0, :, :, cols(c)].reshape(group, CHUNK)
            cts = rows[k : k + count, 1, :, :, cols(c)].reshape(group, CHUNK)
            accs[0, :group] += nt(tok, pair[0, :, cols(c)])
            accs[1, :group] += nt(tok, pair[1, :, cols(c)])
            accs[2, :group] += nt(cts, down[:, cols(c)])
            return carry

        lax.fori_loop(0, chunks, ahead, 0)
        pre_gate, pre_up, hidden_grad = accs[0, :group], accs[1, :group], accs[2, :group]
        sig = jax.nn.sigmoid(pre_gate)
        activated = pre_gate * sig
        hidden = (activated * pre_up).astype(BF16)
        gate_grad = (hidden_grad * pre_up * sig * (1.0 + pre_gate * (1.0 - sig))).astype(BF16)
        up_grad = (hidden_grad * activated).astype(BF16)
        span = slice(k * per_slab, (k + count) * per_slab)
        gate_t[span, :] = gate_grad
        up_t[span, :] = up_grad
        hid_t[span, :] = hidden

        def behind(c, carry):
            got = nn(gate_grad, pair[0, :, cols(c)]) + nn(up_grad, pair[1, :, cols(c)])
            got = got.reshape(count, NY, SLAB, CHUNK)
            own[k : k + count, :, cols(c)] = got[:, 0]
            part[k : k + count, :, :, cols(c)] = got[:, 1:].astype(BF16)
            return carry

        for h in halves:
            over(h, behind)
            for i in range(count):
                give(k + i, h)

    rl_copies = {}
    ru_copies = {}
    rd_copies = {}

    def to_upper(k, h):
        copy = remote(
            part.at[k, 0, :, piece(h)],
            from_down.at[k, :, piece(h)],
            rd_send.at[h, k],
            rd_recv.at[h, k],
            up,
        )
        copy.start()
        rd_copies[k, h] = copy

    def to_lower(k, h):
        copy = remote(
            part.at[k, 2, :, piece(h)],
            from_up.at[k, :, piece(h)],
            ru_send.at[h, k],
            ru_recv.at[h, k],
            dn,
        )
        copy.start()
        ru_copies[k, h] = copy

    def give(k, h):
        copy = remote(
            part.at[k, 1, :, piece(h)],
            relayed.at[k, :, piece(h)],
            rl_send.at[h, k],
            rl_recv.at[h, k],
            (up, dn)[k % 2],
        )
        copy.start()
        rl_copies[k, h] = copy
        (to_lower, to_upper)[k % 2](k, h)

    def give_on(k, h):
        rl_copies[k, h].wait_recv()
        mine = (0, 2)[k % 2]

        def add(c, carry):
            total = part[k, mine, :, cols(c)].astype(F32) + relayed[k, :, cols(c)].astype(F32)
            part[k, mine, :, cols(c)] = total.astype(BF16)
            return carry

        over(h, add)
        (to_upper, to_lower)[k % 2](k, h)

    rz_copies = {}

    def settle(k, h):
        ru_copies[k, h].wait_recv()
        rd_copies[k, h].wait_recv()
        target = back if k == 0 else summed

        def add(c, carry):
            total = own[k, :, cols(c)] + (
                from_up[k, :, cols(c)].astype(F32) + from_down[k, :, cols(c)].astype(F32)
            )
            target[k, :, cols(c)] = total.astype(BF16)
            return carry

        over(h, add)
        if k:
            copy = remote(
                summed.at[k, :, piece(h)],
                back.at[k, :, piece(h)],
                rz_send.at[h, k],
                rz_recv.at[h, k],
                at_z(NZ - OFFSETS[k]),
            )
            copy.start()
            rz_copies[k, h] = copy

    def weight_grads(which):
        def one(c, carry):
            kind = 0 if which < 2 else 1
            data = rows[:, kind, :, :, cols(c)].reshape(NZ * per_slab, CHUNK)
            got = tn((gate_t, up_t, hid_t)[which][...], data).astype(BF16)
            if which < 2:
                gpair[which, :, cols(c)] = got
            else:
                gdown[:, cols(c)] = got
            return carry

        lax.fori_loop(0, chunks, one, 0)
        if which < 2:
            copy = pltpu.make_async_copy(gpair.at[which], gpair_hbm.at[which], store_sem.at[which])
        else:
            copy = pltpu.make_async_copy(gdown, gdown_hbm, store_sem.at[which])
        copy.start()
        return copy

    own_copy.wait()
    cross(0)
    for k in (1, 2, 3):
        spread(k, 0)
    forward(0, 0)
    relay(0, 0)
    forward(1, 0)
    cross(1)
    for k in (1, 2, 3):
        spread(k, 1)
    forward(0, 1)
    for k in (4, 5, 6, 7):
        spread(k, 0)
        spread(k, 1)
    forward(2, 0)
    relay(1, 0)
    forward(1, 1)
    relay(0, 1)
    forward(3, 0)
    relay(2, 0)
    forward(2, 1)
    relay(1, 1)
    forward(3, 1)
    relay(3, 0)
    relay(2, 1)
    loads[2].wait()
    loads[3].wait()

    def both(do, *slabs):
        for k in slabs:
            for h in halves:
                do(k, h)

    both(forward, 4)
    arrived(0)
    arrived(1)
    compute(0, 2)
    relay(3, 1)
    both(relay, 4)
    both(forward, 5)
    both(give_on, 0, 1)
    both(relay, 5)
    both(forward, 6)
    arrived(2)
    arrived(3)
    compute(2, 2)
    both(settle, 0, 1)
    both(relay, 6)
    both(forward, 7)
    both(give_on, 2, 3)
    arrived(4)
    arrived(5)
    compute(4, 2)
    both(settle, 2, 3)
    both(relay, 7)
    both(give_on, 4, 5)
    arrived(6)
    compute(6, 1)
    both(settle, 4, 5)
    arrived(7)
    compute(7, 1)
    both(give_on, 6)
    both(settle, 6)
    stores = [weight_grads(0)]
    both(give_on, 7)
    stores.append(weight_grads(1))
    both(settle, 7)
    stores.append(weight_grads(2))

    half = NXC * NZL * CAP
    qrow = lax.broadcasted_iota(jnp.int32, (half, half), 0)
    qcol = lax.broadcasted_iota(jnp.int32, (half, half), 1)
    q_src = lax.div(qrow, NZL * CAP)
    q_off = lax.rem(lax.div(qrow, CAP), NZL)
    wanted_back = q_off * SLAB + q_src * CAP + lax.rem(qrow, CAP)
    shuffle_back = jnp.where(qcol == wanted_back, 1.0, 0.0).astype(BF16)

    def join(c, carry):
        parts = []
        for i in range(NZL):
            first, second = OFFSETS.index(i), OFFSETS.index(i + NZL)
            total = back[first, :, cols(c)].astype(F32) + back[second, :, cols(c)].astype(F32)
            parts.append(total.astype(BF16))
        moved = nn(shuffle_back, jnp.concatenate(parts, axis=0))
        for i in range(NXC):
            xsend[i, :, cols(c)] = moved[i * NZL * CAP : (i + 1) * NZL * CAP].astype(BF16)
        return carry

    rx_copies = []
    own_back = []
    for h in halves:
        for k in range(1, NZ):
            rz_copies[k, h].wait_recv()
        over(h, join)
        for i in range(1, NXC):
            copy = remote(
                xsend.at[i, :, piece(h)],
                final.at[xc, :, piece(h)],
                rx_send.at[h, i],
                rx_recv.at[h, i],
                at_x(NXC - i),
            )
            copy.start()
            rx_copies.append(copy)
        copy = pltpu.make_async_copy(
            xsend.at[0, :, piece(h)], final.at[xc, :, piece(h)], store_sem.at[3 + h]
        )
        copy.start()
        own_back.append(copy)

    for table in (x_copies, z_copies, y_copies, f_copies, rl_copies, ru_copies, rd_copies, rz_copies):
        for copy in table.values():
            copy.wait_send()
    for copy in rx_copies:
        copy.wait()
    for copy in stores + own_back:
        copy.wait()


def per_device(activations, cotangent, expert_ids, gate_probs, gate_up, down_proj):
    tokens, width = activations.shape
    units = down_proj.shape[1]
    pair = jnp.swapaxes(gate_up[0], 1, 2)
    down = down_proj[0]
    dma = pltpu.SemaphoreType.DMA
    vmem = pltpu.VMEM
    any_space = pl.BlockSpec(memory_space=pl.ANY)
    in_vmem = pl.BlockSpec(memory_space=pltpu.VMEM)
    total_rows = NZ * NY * SLAB
    pick, final, gpair, gdown = pl.pallas_call(
        kernel,
        out_shape=(
            jax.ShapeDtypeStruct((NXC * NZL * CAP, tokens), BF16),
            jax.ShapeDtypeStruct((NXC, NZL * CAP, width), BF16),
            jax.ShapeDtypeStruct((2, units, width), BF16),
            jax.ShapeDtypeStruct((units, width), BF16),
        ),
        in_specs=[in_vmem, in_vmem, any_space, any_space, any_space, any_space],
        out_specs=(in_vmem, any_space, any_space, any_space),
        scratch_shapes=[
            vmem((tokens, width), BF16),
            vmem((tokens, width), BF16),
            vmem((2, units, width), BF16),
            vmem((units, width), BF16),
            vmem((NXC, 2 * NZL * CAP, width), BF16),
            vmem((NXC, 2 * NZL * CAP, width), BF16),
            vmem((NZL, 2, SLAB, width), BF16),
            vmem((NZ, 2, NY, SLAB, width), BF16),
            vmem((3, 2 * NY * SLAB, units), F32),
            vmem((total_rows, units), BF16),
            vmem((total_rows, units), BF16),
            vmem((total_rows, units), BF16),
            vmem((NZ, SLAB, width), F32),
            vmem((NZ, NY - 1, SLAB, width), BF16),
            vmem((NZ, SLAB, width), BF16),
            vmem((NZ, SLAB, width), BF16),
            vmem((NZ, SLAB, width), BF16),
            vmem((NZ, SLAB, width), BF16),
            vmem((NZ, SLAB, width), BF16),
            vmem((NXC, NZL * CAP, width), BF16),
            vmem((2, units, width), BF16),
            vmem((units, width), BF16),
            dma((5,)),
            dma((5,)),
            dma((HALVES, NXC)),
            dma((HALVES, NXC)),
            dma((HALVES, NZ)),
            dma((HALVES, NZ)),
            dma((2, HALVES, NZ)),
            dma((2, HALVES, NZ)),
            dma((HALVES, NZ)),
            dma((HALVES, NZ)),
            dma((HALVES, NZ)),
            dma((HALVES, NZ)),
            dma((HALVES, NZ)),
            dma((HALVES, NZ)),
            dma((HALVES, NZ)),
            dma((HALVES, NZ)),
            dma((HALVES, NZ)),
            dma((HALVES, NZ)),
            dma((HALVES, NXC)),
            dma((HALVES, NXC)),
        ],
        compiler_params=pltpu.CompilerParams(
            collective_id=0, has_side_effects=True, vmem_limit_bytes=60 * 1024 * 1024
        ),
    )(expert_ids.reshape(1, tokens), gate_probs.reshape(1, tokens), activations, cotangent, pair, down)
    out = tn(pick, final.reshape(NXC * NZL * CAP, width)).astype(BF16)
    return out, jnp.swapaxes(gpair, 1, 2)[None], gdown[None]


def solution(mesh):
    in_specs = (
        P(("dp", "expert"), None),
        P(("dp", "expert"), None),
        P(("dp", "expert"), None),
        P(("dp", "expert"), None),
        P("expert", None, None, "dp"),
        P("expert", "dp", None),
    )
    out_specs = (P(("dp", "expert"), None), P("expert", None, None, "dp"), P("expert", "dp", None))
    return jax.shard_map(
        per_device, mesh=mesh, in_specs=in_specs, out_specs=out_specs, check_vma=False
    )
```

```python
import jax
import jax.numpy as jnp
from jax import lax
from jax.experimental import pallas as pl
from jax.experimental.pallas import tpu as pltpu
from jax.sharding import PartitionSpec as P

CAP = 2
MESH = pl.DeviceIdType.MESH
F32 = jnp.float32
BF16 = jnp.bfloat16

NY = 4
NZH = 2
NZL = 4
NZ = NZH * NZL
NXC = 8
SLAB = NXC * CAP
OFFSETS = (0, 1, 7, 2, 6, 3, 5, 4)
CHUNK = 512
X_PIECES = 4
OUT_PIECES = (4, 2, 2, 2, 2, 2, 2, 2)
BACK_PIECES = (2, 2, 2, 2, 2, 2, 2, 2)
END_PIECES = 2
MOST = 4
ORDER = (
    ('cross', 0),
    ('forward', 0, 0),
    ('cross', 1),
    ('spread', 3, 0),
    ('forward', 0, 1),
    ('spread', 2, 0),
    ('cross', 2),
    ('spread', 1, 0),
    ('spread', 6, 0),
    ('spread', 4, 0),
    ('spread', 5, 0),
    ('forward', 0, 2),
    ('relay', 0, 1),
    ('cross', 3),
    ('forward', 0, 3),
    ('spread', 2, 1),
    ('forward', 2, 0),
    ('spread', 5, 1),
    ('relay', 0, 0),
    ('forward', 3, 0),
    ('spread', 1, 1),
    ('forward', 1, 0),
    ('relay', 3, 0),
    ('relay', 0, 2),
    ('relay', 2, 0),
    ('spread', 4, 1),
    ('spread', 7, 0),
    ('spread', 6, 1),
    ('relay', 1, 0),
    ('forward', 4, 0),
    ('forward', 2, 1),
    ('relay', 0, 3),
    ('forward', 6, 0),
    ('forward', 5, 0),
    ('forward', 4, 1),
    ('relay', 2, 1),
    ('forward', 5, 1),
    ('relay', 4, 0),
    ('relay', 5, 0),
    ('spread', 7, 1),
    ('forward', 1, 1),
    ('relay', 5, 1),
    ('relay', 4, 1),
    ('forward', 7, 0),
    ('spread', 3, 1),
    ('relay', 1, 1),
    ('forward', 6, 1),
    ('relay', 6, 0),
    ('forward', 7, 1),
    ('relay', 7, 0),
    ('relay', 7, 1),
    ('relay', 6, 1),
    ('forward', 3, 1),
    ('compute', 4, 2),
    ('compute', 6, 2),
    ('give_on', 4, 0),
    ('give_on', 5, 0),
    ('give_on', 7, 0),
    ('relay', 3, 1),
    ('give_on', 5, 1),
    ('give_on', 6, 0),
    ('compute', 0, 2),
    ('give_on', 6, 1),
    ('settle', 5, 0),
    ('settle', 4, 0),
    ('give_on', 4, 1),
    ('give_on', 7, 1),
    ('settle', 7, 0),
    ('settle', 6, 0),
    ('compute', 2, 2),
    ('grads', 2),
    ('settle', 4, 1),
    ('give_on', 0, 1),
    ('settle', 5, 1),
    ('give_on', 3, 0),
    ('settle', 7, 1),
    ('settle', 6, 1),
    ('give_on', 0, 0),
    ('give_on', 1, 0),
    ('give_on', 2, 0),
    ('give_on', 2, 1),
    ('give_on', 3, 1),
    ('give_on', 1, 1),
    ('settle', 3, 0),
    ('settle', 1, 0),
    ('settle', 0, 1),
    ('settle', 2, 0),
    ('settle', 0, 0),
    ('settle', 3, 1),
    ('settle', 1, 1),
    ('settle', 2, 1),
    ('join', 0),
    ('grads', 0),
    ('join', 1),
    ('grads', 1),
)


def nt(left, right):
    return lax.dot_general(left, right, (((1,), (1,)), ((), ())), preferred_element_type=F32)


def nn(left, right):
    return lax.dot_general(left, right, (((1,), (0,)), ((), ())), preferred_element_type=F32)


def tn(left, right):
    return lax.dot_general(left, right, (((0,), (0,)), ((), ())), preferred_element_type=F32)


def kernel(
    ids_ref,
    probs_ref,
    act_hbm,
    cot_hbm,
    pair_hbm,
    down_hbm,
    pick_ref,
    final,
    gpair,
    gdown,
    act,
    cot,
    pair,
    down,
    send,
    recv1,
    perm,
    rows,
    accs,
    gate_t,
    up_t,
    hid_t,
    own,
    part,
    relayed,
    from_up,
    from_down,
    summed,
    back,
    xsend,
    load_sem,
    store_sem,
    x_send,
    x_recv,
    z_send,
    z_recv,
    y_send,
    y_recv,
    f_send,
    f_recv,
    rl_send,
    rl_recv,
    ru_send,
    ru_recv,
    rd_send,
    rd_recv,
    rz_send,
    rz_recv,
    rx_send,
    rx_recv,
):
    width = act.shape[1]
    chunks = width // CHUNK
    tokens = act.shape[0]
    e = lax.axis_index("expert")
    d = lax.axis_index("dp")
    zl = lax.div(e, NXC)
    xc = lax.rem(e, NXC)
    y = lax.div(d, NZH)
    z = lax.rem(d, NZH) * NZL + zl

    def dev(yy, zz, xx):
        return (yy * NZH + lax.div(zz, NZL), lax.rem(zz, NZL) * NXC + xx)

    def at_x(i):
        return dev(y, z, lax.rem(xc + i, NXC))

    def at_z(i):
        return dev(y, lax.rem(z + i, NZ), xc)

    up = dev(lax.rem(y + 1, NY), z, xc)
    dn = dev(lax.rem(y + NY - 1, NY), z, xc)

    def cols(c):
        return pl.ds(pl.multiple_of(c * CHUNK, CHUNK), CHUNK)

    def piece(count, h):
        return pl.ds(h * (width // count), width // count)

    def over(count, h, body):
        lax.fori_loop(h * chunks // count, (h + 1) * chunks // count, body, 0)

    def remote(src, dst, ssem, rsem, where):
        return pltpu.make_async_remote_copy(
            src_ref=src, dst_ref=dst, send_sem=ssem, recv_sem=rsem, device_id=where, device_id_type=MESH
        )

    loads = [
        pltpu.make_async_copy(act_hbm, act, load_sem.at[0]),
        pltpu.make_async_copy(cot_hbm, cot, load_sem.at[1]),
        pltpu.make_async_copy(pair_hbm, pair, load_sem.at[2]),
        pltpu.make_async_copy(down_hbm, down, load_sem.at[3]),
    ]
    for copy in loads:
        copy.start()
    barrier = pltpu.get_barrier_semaphore()
    far_first = (4, 3, 5, 2, 6, 1, 7)
    partners = [at_z(i) for i in far_first] + [at_x(i) for i in (4, 5, 2, 3, 6, 7, 1)] + [up, dn]
    for partner in partners:
        pl.semaphore_signal(barrier, inc=1, device_id=partner, device_id_type=MESH)

    ids = ids_ref[...]
    ids_wide = jnp.broadcast_to(ids.astype(F32), (tokens, tokens))
    ids_tall = ids_wide.T
    row_at = lax.broadcasted_iota(jnp.int32, (tokens, tokens), 0)
    col_at = lax.broadcasted_iota(jnp.int32, (tokens, tokens), 1)
    earlier = jnp.where((ids_wide == ids_tall) & (row_at < col_at), 1.0, 0.0)
    rank = jnp.sum(earlier, axis=0, keepdims=True).astype(jnp.int32)
    offset = lax.rem(lax.div(ids, NXC) + NZL - zl, NZL)
    inside = ids < NZL * NXC
    place = lax.rem(ids, NXC) * (2 * NZL * CAP) + offset * CAP + rank
    place = jnp.where(inside, place, -1024)
    pick_tok = jnp.where(row_at == place, 1.0, 0.0).astype(BF16)
    pick_cot = jnp.where(row_at == place + NZL * CAP, 1.0, 0.0).astype(BF16)
    slot = lax.rem(ids, NXC) * (NZL * CAP) + offset * CAP + rank
    slot = jnp.where(inside, slot, -1024)
    half_row = lax.broadcasted_iota(jnp.int32, (NXC * NZL * CAP, tokens), 0)
    pick_ref[...] = jnp.where(half_row == slot, 1.0, 0.0).astype(BF16)

    loads[0].wait()
    loads[1].wait()
    probs = jnp.broadcast_to(probs_ref[...], (tokens, tokens)).T[:, :1]

    def gather_rows(c, carry):
        scaled = (probs * cot[:, cols(c)].astype(F32)).astype(BF16)
        got = nn(pick_tok, act[:, cols(c)]) + nn(pick_cot, scaled)
        got = got.astype(BF16).reshape(NXC, 2 * NZL * CAP, CHUNK)
        send[:, :, cols(c)] = got
        return carry

    lax.fori_loop(0, chunks, gather_rows, 0)
    pl.semaphore_wait(barrier, len(partners))

    x_copies = {}
    for h in range(X_PIECES):
        for i in range(1, NXC):
            copy = remote(
                send.at[lax.rem(xc + i, NXC), :, piece(X_PIECES, h)],
                recv1.at[i, :, piece(X_PIECES, h)],
                x_send.at[h, i],
                x_recv.at[h, i],
                at_x(i),
            )
            copy.start()
            x_copies[h, i] = copy
    own_copy = pltpu.make_async_copy(send.at[xc], recv1.at[0], load_sem.at[4])
    own_copy.start()

    prow = lax.broadcasted_iota(jnp.int32, (2 * NXC * NZL * CAP, 2 * NXC * NZL * CAP), 0)
    pcol = lax.broadcasted_iota(jnp.int32, (2 * NXC * NZL * CAP, 2 * NXC * NZL * CAP), 1)
    p_off = lax.div(prow, 2 * SLAB)
    p_kind = lax.rem(lax.div(prow, SLAB), 2)
    p_src = lax.rem(lax.div(prow, CAP), NXC)
    p_rank = lax.rem(prow, CAP)
    wanted = p_src * (2 * NZL * CAP) + p_kind * (NZL * CAP) + p_off * CAP + p_rank
    shuffle = jnp.where(pcol == wanted, 1.0, 0.0).astype(BF16)

    def shuffle_rows(c, carry):
        got = recv1[:, :, cols(c)].reshape(2 * NXC * NZL * CAP, CHUNK)
        moved = nn(shuffle, got).astype(BF16).reshape(NZL, 2, SLAB, CHUNK)
        perm[:, :, :, cols(c)] = moved
        rows[0, :, 0, :, cols(c)] = moved[0]
        return carry

    def cross(h):
        if h == 0:
            own_copy.wait()
        for i in range(1, NXC):
            x_copies[h, i].wait_recv()
        over(X_PIECES, h, shuffle_rows)

    z_copies = {}

    def spread(k, h):
        copy = remote(
            perm.at[OFFSETS[k] % NZL, :, :, piece(OUT_PIECES[k], h)],
            rows.at[k, :, 0, :, piece(OUT_PIECES[k], h)],
            z_send.at[h, k],
            z_recv.at[h, k],
            at_z(OFFSETS[k]),
        )
        copy.start()
        z_copies[k, h] = copy

    y_copies = {}
    f_copies = {}

    def forward(k, h):
        if k:
            z_copies[k, h].wait_recv()
        for way, (where, there) in enumerate(((up, 3), (dn, 1))):
            copy = remote(
                rows.at[k, :, 0, :, piece(OUT_PIECES[k], h)],
                rows.at[k, :, there, :, piece(OUT_PIECES[k], h)],
                y_send.at[way, h, k],
                y_recv.at[way, h, k],
                where,
            )
            copy.start()
            y_copies[way, k, h] = copy

    def relay(k, h):
        way = k % 2
        y_copies[way, k, h].wait_recv()
        mine, where = ((3, up), (1, dn))[way]
        copy = remote(
            rows.at[k, :, mine, :, piece(OUT_PIECES[k], h)],
            rows.at[k, :, 2, :, piece(OUT_PIECES[k], h)],
            f_send.at[h, k],
            f_recv.at[h, k],
            where,
        )
        copy.start()
        f_copies[k, h] = copy

    def arrived(k):
        for h in range(OUT_PIECES[k]):
            y_copies[1 - k % 2, k, h].wait_recv()
            f_copies[k, h].wait_recv()

    per_slab = NY * SLAB

    def compute(k, count):
        for i in range(count):
            arrived(k + i)
        group = count * per_slab
        accs[:, :group] = jnp.zeros((3, group, accs.shape[2]), F32)

        def ahead(c, carry):
            tok = rows[k : k + count, 0, :, :, cols(c)].reshape(group, CHUNK)
            cts = rows[k : k + count, 1, :, :, cols(c)].reshape(group, CHUNK)
            accs[0, :group] += nt(tok, pair[0, :, cols(c)])
            accs[1, :group] += nt(tok, pair[1, :, cols(c)])
            accs[2, :group] += nt(cts, down[:, cols(c)])
            return carry

        lax.fori_loop(0, chunks, ahead, 0)
        pre_gate, pre_up, hidden_grad = accs[0, :group], accs[1, :group], accs[2, :group]
        sig = jax.nn.sigmoid(pre_gate)
        activated = pre_gate * sig
        hidden = (activated * pre_up).astype(BF16)
        gate_grad = (hidden_grad * pre_up * sig * (1.0 + pre_gate * (1.0 - sig))).astype(BF16)
        up_grad = (hidden_grad * activated).astype(BF16)
        span = slice(k * per_slab, (k + count) * per_slab)
        gate_t[span, :] = gate_grad
        up_t[span, :] = up_grad
        hid_t[span, :] = hidden

        def behind(c, carry):
            got = nn(gate_grad, pair[0, :, cols(c)]) + nn(up_grad, pair[1, :, cols(c)])
            got = got.reshape(count, NY, SLAB, CHUNK)
            own[k : k + count, :, cols(c)] = got[:, 0]
            part[k : k + count, :, :, cols(c)] = got[:, 1:].astype(BF16)
            return carry

        for h in range(BACK_PIECES[k]):
            over(BACK_PIECES[k], h, behind)
            for i in range(count):
                give(k + i, h)

    rl_copies = {}
    ru_copies = {}
    rd_copies = {}

    def to_upper(k, h):
        copy = remote(
            part.at[k, 0, :, piece(BACK_PIECES[k], h)],
            from_down.at[k, :, piece(BACK_PIECES[k], h)],
            rd_send.at[h, k],
            rd_recv.at[h, k],
            up,
        )
        copy.start()
        rd_copies[k, h] = copy

    def to_lower(k, h):
        copy = remote(
            part.at[k, 2, :, piece(BACK_PIECES[k], h)],
            from_up.at[k, :, piece(BACK_PIECES[k], h)],
            ru_send.at[h, k],
            ru_recv.at[h, k],
            dn,
        )
        copy.start()
        ru_copies[k, h] = copy

    def give(k, h):
        copy = remote(
            part.at[k, 1, :, piece(BACK_PIECES[k], h)],
            relayed.at[k, :, piece(BACK_PIECES[k], h)],
            rl_send.at[h, k],
            rl_recv.at[h, k],
            (up, dn)[k % 2],
        )
        copy.start()
        rl_copies[k, h] = copy
        (to_lower, to_upper)[k % 2](k, h)

    def give_on(k, h):
        rl_copies[k, h].wait_recv()
        mine = (0, 2)[k % 2]

        def add(c, carry):
            total = part[k, mine, :, cols(c)].astype(F32) + relayed[k, :, cols(c)].astype(F32)
            part[k, mine, :, cols(c)] = total.astype(BF16)
            return carry

        over(BACK_PIECES[k], h, add)
        (to_upper, to_lower)[k % 2](k, h)

    rz_copies = {}

    def settle(k, h):
        ru_copies[k, h].wait_recv()
        rd_copies[k, h].wait_recv()
        target = back if k == 0 else summed

        def add(c, carry):
            total = own[k, :, cols(c)] + (
                from_up[k, :, cols(c)].astype(F32) + from_down[k, :, cols(c)].astype(F32)
            )
            target[k, :, cols(c)] = total.astype(BF16)
            return carry

        over(BACK_PIECES[k], h, add)
        if k:
            copy = remote(
                summed.at[k, :, piece(BACK_PIECES[k], h)],
                back.at[k, :, piece(BACK_PIECES[k], h)],
                rz_send.at[h, k],
                rz_recv.at[h, k],
                at_z(NZ - OFFSETS[k]),
            )
            copy.start()
            rz_copies[k, h] = copy

    def grads(which):
        def one(c, carry):
            kind = 0 if which < 2 else 1
            data = rows[:, kind, :, :, cols(c)].reshape(NZ * per_slab, CHUNK)
            got = tn((gate_t, up_t, hid_t)[which][...], data).astype(BF16)
            if which < 2:
                gpair[which, :, cols(c)] = got
            else:
                gdown[:, cols(c)] = got
            return carry

        lax.fori_loop(0, chunks, one, 0)
    half = NXC * NZL * CAP
    qrow = lax.broadcasted_iota(jnp.int32, (half, half), 0)
    qcol = lax.broadcasted_iota(jnp.int32, (half, half), 1)
    q_src = lax.div(qrow, NZL * CAP)
    q_off = lax.rem(lax.div(qrow, CAP), NZL)
    wanted_back = q_off * SLAB + q_src * CAP + lax.rem(qrow, CAP)
    shuffle_back = jnp.where(qcol == wanted_back, 1.0, 0.0).astype(BF16)

    def add_halves(c, carry):
        parts = []
        for i in range(NZL):
            first, second = OFFSETS.index(i), OFFSETS.index(i + NZL)
            total = back[first, :, cols(c)].astype(F32) + back[second, :, cols(c)].astype(F32)
            parts.append(total.astype(BF16))
        moved = nn(shuffle_back, jnp.concatenate(parts, axis=0))
        for i in range(NXC):
            xsend[i, :, cols(c)] = moved[i * NZL * CAP : (i + 1) * NZL * CAP].astype(BF16)
        return carry

    rx_copies = []
    own_back = []

    def join(h):
        for k in range(1, NZ):
            for q in range(BACK_PIECES[k]):
                if q * END_PIECES < (h + 1) * BACK_PIECES[k] and (q + 1) * END_PIECES > h * BACK_PIECES[k]:
                    if (k, q) not in taken:
                        rz_copies[k, q].wait_recv()
                        taken.add((k, q))
        over(END_PIECES, h, add_halves)
        for i in range(1, NXC):
            copy = remote(
                xsend.at[i, :, piece(END_PIECES, h)],
                final.at[xc, :, piece(END_PIECES, h)],
                rx_send.at[h, i],
                rx_recv.at[h, i],
                at_x(NXC - i),
            )
            copy.start()
            rx_copies.append(copy)
        copy = pltpu.make_async_copy(
            xsend.at[0, :, piece(END_PIECES, h)], final.at[xc, :, piece(END_PIECES, h)], store_sem.at[h]
        )
        copy.start()
        own_back.append(copy)

    taken = set()
    loads[2].wait()
    loads[3].wait()
    steps = {
        "cross": cross,
        "spread": spread,
        "forward": forward,
        "relay": relay,
        "compute": compute,
        "give_on": give_on,
        "settle": settle,
        "grads": grads,
        "join": join,
    }
    for name, *where in ORDER:
        steps[name](*where)

    for table in (x_copies, z_copies, y_copies, f_copies, rl_copies, ru_copies, rd_copies, rz_copies):
        for copy in table.values():
            copy.wait_send()
    for copy in rx_copies:
        copy.wait()
    for copy in own_back:
        copy.wait()


def per_device(activations, cotangent, expert_ids, gate_probs, gate_up, down_proj):
    tokens, width = activations.shape
    units = down_proj.shape[1]
    pair = jnp.swapaxes(gate_up[0], 1, 2)
    down = down_proj[0]
    dma = pltpu.SemaphoreType.DMA
    vmem = pltpu.VMEM
    any_space = pl.BlockSpec(memory_space=pl.ANY)
    in_vmem = pl.BlockSpec(memory_space=pltpu.VMEM)
    total_rows = NZ * NY * SLAB
    pick, final, gpair, gdown = pl.pallas_call(
        kernel,
        out_shape=(
            jax.ShapeDtypeStruct((NXC * NZL * CAP, tokens), BF16),
            jax.ShapeDtypeStruct((NXC, NZL * CAP, width), BF16),
            pltpu.VMEM((2, units, width), BF16),
            pltpu.VMEM((units, width), BF16),
        ),
        in_specs=[in_vmem, in_vmem, any_space, any_space, any_space, any_space],
        out_specs=(in_vmem, any_space, in_vmem, in_vmem),
        scratch_shapes=[
            vmem((tokens, width), BF16),
            vmem((tokens, width), BF16),
            vmem((2, units, width), BF16),
            vmem((units, width), BF16),
            vmem((NXC, 2 * NZL * CAP, width), BF16),
            vmem((NXC, 2 * NZL * CAP, width), BF16),
            vmem((NZL, 2, SLAB, width), BF16),
            vmem((NZ, 2, NY, SLAB, width), BF16),
            vmem((3, 2 * NY * SLAB, units), F32),
            vmem((total_rows, units), BF16),
            vmem((total_rows, units), BF16),
            vmem((total_rows, units), BF16),
            vmem((NZ, SLAB, width), F32),
            vmem((NZ, NY - 1, SLAB, width), BF16),
            vmem((NZ, SLAB, width), BF16),
            vmem((NZ, SLAB, width), BF16),
            vmem((NZ, SLAB, width), BF16),
            vmem((NZ, SLAB, width), BF16),
            vmem((NZ, SLAB, width), BF16),
            vmem((NXC, NZL * CAP, width), BF16),
            dma((5,)),
            dma((5,)),
            dma((X_PIECES, NXC)),
            dma((X_PIECES, NXC)),
            dma((MOST, NZ)),
            dma((MOST, NZ)),
            dma((2, MOST, NZ)),
            dma((2, MOST, NZ)),
            dma((MOST, NZ)),
            dma((MOST, NZ)),
            dma((MOST, NZ)),
            dma((MOST, NZ)),
            dma((MOST, NZ)),
            dma((MOST, NZ)),
            dma((MOST, NZ)),
            dma((MOST, NZ)),
            dma((MOST, NZ)),
            dma((MOST, NZ)),
            dma((END_PIECES, NXC)),
            dma((END_PIECES, NXC)),
        ],
        compiler_params=pltpu.CompilerParams(
            collective_id=0, has_side_effects=True, vmem_limit_bytes=48 * 1024 * 1024
        ),
    )(expert_ids.reshape(1, tokens), gate_probs.reshape(1, tokens), activations, cotangent, pair, down)
    out = tn(pick, final.reshape(NXC * NZL * CAP, width)).astype(BF16)
    return out, jnp.swapaxes(gpair, 1, 2)[None], gdown[None]


def solution(mesh):
    in_specs = (
        P(("dp", "expert"), None),
        P(("dp", "expert"), None),
        P(("dp", "expert"), None),
        P(("dp", "expert"), None),
        P("expert", None, None, "dp"),
        P("expert", "dp", None),
    )
    out_specs = (P(("dp", "expert"), None), P("expert", None, None, "dp"), P("expert", "dp", None))
    return jax.shard_map(
        per_device, mesh=mesh, in_specs=in_specs, out_specs=out_specs, check_vma=False
    )
```

```python
import jax
import jax.numpy as jnp
from jax import lax
from jax.experimental import pallas as pl
from jax.experimental.pallas import tpu as pltpu
from jax.sharding import PartitionSpec as P

CAP = 2
MESH = pl.DeviceIdType.MESH
F32 = jnp.float32
BF16 = jnp.bfloat16

NY = 4
NZH = 2
NZL = 4
NZ = NZH * NZL
NXC = 8
SLAB = NXC * CAP
OFFSETS = (0, 1, 6, 2, 4, 5, 3, 7)
CHUNK = 512
X_PIECES = 8
OUT_PIECES = (4, 4, 4, 2, 2, 2, 2, 2)
BACK_PIECES = (2, 2, 2, 2, 2, 2, 4, 4)
END_PIECES = 4
MOST = 4
ORDER = (
    ('cross', 0),
    ('cross', 1),
    ('spread', 1, 0),
    ('spread', 2, 0),
    ('forward', 0, 0),
    ('cross', 2),
    ('cross', 3),
    ('spread', 1, 1),
    ('forward', 0, 1),
    ('spread', 3, 0),
    ('spread', 7, 0),
    ('relay', 0, 0),
    ('cross', 4),
    ('spread', 5, 0),
    ('cross', 5),
    ('forward', 0, 2),
    ('forward', 1, 0),
    ('cross', 6),
    ('cross', 7),
    ('forward', 0, 3),
    ('forward', 1, 1),
    ('spread', 1, 3),
    ('spread', 1, 2),
    ('spread', 3, 1),
    ('spread', 7, 1),
    ('relay', 0, 2),
    ('spread', 4, 0),
    ('forward', 2, 0),
    ('forward', 7, 0),
    ('spread', 4, 1),
    ('relay', 1, 1),
    ('forward', 1, 3),
    ('spread', 6, 1),
    ('forward', 3, 0),
    ('forward', 5, 0),
    ('spread', 2, 2),
    ('forward', 1, 2),
    ('spread', 6, 0),
    ('forward', 3, 1),
    ('relay', 5, 0),
    ('forward', 7, 1),
    ('relay', 7, 0),
    ('spread', 2, 1),
    ('relay', 1, 3),
    ('relay', 2, 0),
    ('relay', 0, 1),
    ('relay', 3, 0),
    ('forward', 4, 0),
    ('spread', 5, 1),
    ('forward', 4, 1),
    ('relay', 4, 0),
    ('spread', 2, 3),
    ('forward', 2, 1),
    ('forward', 2, 2),
    ('relay', 4, 1),
    ('relay', 0, 3),
    ('forward', 5, 1),
    ('relay', 3, 1),
    ('forward', 6, 1),
    ('relay', 5, 1),
    ('forward', 2, 3),
    ('relay', 7, 1),
    ('forward', 6, 0),
    ('relay', 6, 1),
    ('relay', 2, 1),
    ('relay', 2, 2),
    ('relay', 2, 3),
    ('relay', 6, 0),
    ('compute', 4, 2),
    ('compute', 2, 2),
    ('give_on', 5, 1),
    ('give_on', 3, 0),
    ('relay', 1, 0),
    ('give_on', 5, 0),
    ('relay', 1, 2),
    ('give_on', 4, 0),
    ('give_on', 4, 1),
    ('compute', 6, 2),
    ('settle', 3, 0),
    ('settle', 4, 0),
    ('settle', 4, 1),
    ('give_on', 6, 0),
    ('give_on', 2, 0),
    ('give_on', 3, 1),
    ('settle', 5, 1),
    ('give_on', 6, 1),
    ('compute', 0, 2),
    ('settle', 5, 0),
    ('settle', 6, 0),
    ('grads', 2),
    ('settle', 3, 1),
    ('give_on', 7, 0),
    ('give_on', 6, 3),
    ('give_on', 2, 1),
    ('give_on', 6, 2),
    ('settle', 6, 1),
    ('give_on', 1, 0),
    ('give_on', 7, 1),
    ('settle', 2, 0),
    ('give_on', 0, 0),
    ('give_on', 0, 1),
    ('give_on', 7, 2),
    ('give_on', 7, 3),
    ('settle', 6, 3),
    ('give_on', 1, 1),
    ('settle', 7, 0),
    ('settle', 2, 1),
    ('settle', 1, 0),
    ('settle', 6, 2),
    ('settle', 7, 1),
    ('grads', 1),
    ('settle', 1, 1),
    ('settle', 7, 3),
    ('settle', 0, 0),
    ('join', 0),
    ('settle', 0, 1),
    ('settle', 7, 2),
    ('join', 1),
    ('join', 3),
    ('join', 2),
    ('grads', 0),
)


def nt(left, right):
    return lax.dot_general(left, right, (((1,), (1,)), ((), ())), preferred_element_type=F32)


def nn(left, right):
    return lax.dot_general(left, right, (((1,), (0,)), ((), ())), preferred_element_type=F32)


def tn(left, right):
    return lax.dot_general(left, right, (((0,), (0,)), ((), ())), preferred_element_type=F32)


def kernel(
    ids_hbm,
    probs_hbm,
    act_hbm,
    cot_hbm,
    pair_hbm,
    down_hbm,
    pick_ref,
    final,
    gpair,
    gdown,
    ids_ref,
    probs_ref,
    act,
    cot,
    pair,
    down,
    send,
    recv1,
    perm,
    rows,
    accs,
    gate_t,
    up_t,
    hid_t,
    own,
    part,
    relayed,
    from_up,
    from_down,
    summed,
    back,
    xsend,
    load_sem,
    store_sem,
    x_send,
    x_recv,
    z_send,
    z_recv,
    y_send,
    y_recv,
    f_send,
    f_recv,
    rl_send,
    rl_recv,
    ru_send,
    ru_recv,
    rd_send,
    rd_recv,
    rz_send,
    rz_recv,
    rx_send,
    rx_recv,
):
    width = act.shape[1]
    chunks = width // CHUNK
    tokens = act.shape[0]
    e = lax.axis_index("expert")
    d = lax.axis_index("dp")
    zl = lax.div(e, NXC)
    xc = lax.rem(e, NXC)
    y = lax.div(d, NZH)
    z = lax.rem(d, NZH) * NZL + zl

    def dev(yy, zz, xx):
        return (yy * NZH + lax.div(zz, NZL), lax.rem(zz, NZL) * NXC + xx)

    def at_x(i):
        return dev(y, z, lax.rem(xc + i, NXC))

    def at_z(i):
        return dev(y, lax.rem(z + i, NZ), xc)

    up = dev(lax.rem(y + 1, NY), z, xc)
    dn = dev(lax.rem(y + NY - 1, NY), z, xc)

    def cols(c):
        return pl.ds(pl.multiple_of(c * CHUNK, CHUNK), CHUNK)

    def piece(count, h):
        return pl.ds(h * (width // count), width // count)

    def over(count, h, body):
        lax.fori_loop(h * chunks // count, (h + 1) * chunks // count, body, 0)

    def remote(src, dst, ssem, rsem, where):
        return pltpu.make_async_remote_copy(
            src_ref=src, dst_ref=dst, send_sem=ssem, recv_sem=rsem, device_id=where, device_id_type=MESH
        )

    loads = [
        pltpu.make_async_copy(act_hbm, act, load_sem.at[0]),
        pltpu.make_async_copy(cot_hbm, cot, load_sem.at[1]),
        pltpu.make_async_copy(pair_hbm, pair, load_sem.at[2]),
        pltpu.make_async_copy(down_hbm, down, load_sem.at[3]),
    ]
    small_loads = [
        pltpu.make_async_copy(ids_hbm, ids_ref, load_sem.at[5]),
        pltpu.make_async_copy(probs_hbm, probs_ref, load_sem.at[6]),
    ]
    for copy in small_loads:
        copy.start()
    for copy in loads:
        copy.start()
    barrier = pltpu.get_barrier_semaphore()
    far_first = (4, 3, 5, 2, 6, 1, 7)
    partners = [at_z(i) for i in far_first] + [at_x(i) for i in (4, 5, 2, 3, 6, 7, 1)] + [up, dn]
    for partner in partners:
        pl.semaphore_signal(barrier, inc=1, device_id=partner, device_id_type=MESH)

    for copy in small_loads:
        copy.wait()
    ids = ids_ref[...]
    ids_wide = jnp.broadcast_to(ids.astype(F32), (tokens, tokens))
    ids_tall = ids_wide.T
    row_at = lax.broadcasted_iota(jnp.int32, (tokens, tokens), 0)
    col_at = lax.broadcasted_iota(jnp.int32, (tokens, tokens), 1)
    earlier = jnp.where((ids_wide == ids_tall) & (row_at < col_at), 1.0, 0.0)
    rank = jnp.sum(earlier, axis=0, keepdims=True).astype(jnp.int32)
    offset = lax.rem(lax.div(ids, NXC) + NZL - zl, NZL)
    inside = ids < NZL * NXC
    place = lax.rem(ids, NXC) * (2 * NZL * CAP) + offset * CAP + rank
    place = jnp.where(inside, place, -1024)
    pick_tok = jnp.where(row_at == place, 1.0, 0.0).astype(BF16)
    pick_cot = jnp.where(row_at == place + NZL * CAP, 1.0, 0.0).astype(BF16)
    slot = lax.rem(ids, NXC) * (NZL * CAP) + offset * CAP + rank
    slot = jnp.where(inside, slot, -1024)
    half_row = lax.broadcasted_iota(jnp.int32, (NXC * NZL * CAP, tokens), 0)
    pick_ref[...] = jnp.where(half_row == slot, 1.0, 0.0).astype(BF16)

    loads[0].wait()
    loads[1].wait()
    probs = jnp.broadcast_to(probs_ref[...], (tokens, tokens)).T[:, :1]

    def gather_rows(c, carry):
        scaled = (probs * cot[:, cols(c)].astype(F32)).astype(BF16)
        got = nn(pick_tok, act[:, cols(c)]) + nn(pick_cot, scaled)
        got = got.astype(BF16).reshape(NXC, 2 * NZL * CAP, CHUNK)
        send[:, :, cols(c)] = got
        return carry

    lax.fori_loop(0, chunks, gather_rows, 0)
    pl.semaphore_wait(barrier, len(partners))

    x_copies = {}
    for h in range(X_PIECES):
        for i in range(1, NXC):
            copy = remote(
                send.at[lax.rem(xc + i, NXC), :, piece(X_PIECES, h)],
                recv1.at[i, :, piece(X_PIECES, h)],
                x_send.at[h, i],
                x_recv.at[h, i],
                at_x(i),
            )
            copy.start()
            x_copies[h, i] = copy
    own_copy = pltpu.make_async_copy(send.at[xc], recv1.at[0], load_sem.at[4])
    own_copy.start()

    prow = lax.broadcasted_iota(jnp.int32, (2 * NXC * NZL * CAP, 2 * NXC * NZL * CAP), 0)
    pcol = lax.broadcasted_iota(jnp.int32, (2 * NXC * NZL * CAP, 2 * NXC * NZL * CAP), 1)
    p_off = lax.div(prow, 2 * SLAB)
    p_kind = lax.rem(lax.div(prow, SLAB), 2)
    p_src = lax.rem(lax.div(prow, CAP), NXC)
    p_rank = lax.rem(prow, CAP)
    wanted = p_src * (2 * NZL * CAP) + p_kind * (NZL * CAP) + p_off * CAP + p_rank
    shuffle = jnp.where(pcol == wanted, 1.0, 0.0).astype(BF16)

    def shuffle_rows(c, carry):
        got = recv1[:, :, cols(c)].reshape(2 * NXC * NZL * CAP, CHUNK)
        moved = nn(shuffle, got).astype(BF16).reshape(NZL, 2, SLAB, CHUNK)
        perm[:, :, :, cols(c)] = moved
        rows[0, :, 0, :, cols(c)] = moved[0]
        return carry

    def cross(h):
        if h == 0:
            own_copy.wait()
        for i in range(1, NXC):
            x_copies[h, i].wait_recv()
        over(X_PIECES, h, shuffle_rows)

    z_copies = {}

    def spread(k, h):
        copy = remote(
            perm.at[OFFSETS[k] % NZL, :, :, piece(OUT_PIECES[k], h)],
            rows.at[k, :, 0, :, piece(OUT_PIECES[k], h)],
            z_send.at[h, k],
            z_recv.at[h, k],
            at_z(OFFSETS[k]),
        )
        copy.start()
        z_copies[k, h] = copy

    y_copies = {}
    f_copies = {}

    def forward(k, h):
        if k:
            z_copies[k, h].wait_recv()
        for way, (where, there) in enumerate(((up, 3), (dn, 1))):
            copy = remote(
                rows.at[k, :, 0, :, piece(OUT_PIECES[k], h)],
                rows.at[k, :, there, :, piece(OUT_PIECES[k], h)],
                y_send.at[way, h, k],
                y_recv.at[way, h, k],
                where,
            )
            copy.start()
            y_copies[way, k, h] = copy

    def relay(k, h):
        way = k % 2
        y_copies[way, k, h].wait_recv()
        mine, where = ((3, up), (1, dn))[way]
        copy = remote(
            rows.at[k, :, mine, :, piece(OUT_PIECES[k], h)],
            rows.at[k, :, 2, :, piece(OUT_PIECES[k], h)],
            f_send.at[h, k],
            f_recv.at[h, k],
            where,
        )
        copy.start()
        f_copies[k, h] = copy

    def arrived(k):
        for h in range(OUT_PIECES[k]):
            y_copies[1 - k % 2, k, h].wait_recv()
            f_copies[k, h].wait_recv()

    per_slab = NY * SLAB

    def compute(k, count):
        for i in range(count):
            arrived(k + i)
        group = count * per_slab
        accs[:, :group] = jnp.zeros((3, group, accs.shape[2]), F32)

        def ahead(c, carry):
            tok = rows[k : k + count, 0, :, :, cols(c)].reshape(group, CHUNK)
            cts = rows[k : k + count, 1, :, :, cols(c)].reshape(group, CHUNK)
            accs[0, :group] += nt(tok, pair[0, :, cols(c)])
            accs[1, :group] += nt(tok, pair[1, :, cols(c)])
            accs[2, :group] += nt(cts, down[:, cols(c)])
            return carry

        lax.fori_loop(0, chunks, ahead, 0)
        pre_gate, pre_up, hidden_grad = accs[0, :group], accs[1, :group], accs[2, :group]
        sig = jax.nn.sigmoid(pre_gate)
        activated = pre_gate * sig
        hidden = (activated * pre_up).astype(BF16)
        gate_grad = (hidden_grad * pre_up * sig * (1.0 + pre_gate * (1.0 - sig))).astype(BF16)
        up_grad = (hidden_grad * activated).astype(BF16)
        span = slice(k * per_slab, (k + count) * per_slab)
        gate_t[span, :] = gate_grad
        up_t[span, :] = up_grad
        hid_t[span, :] = hidden

        def behind(c, carry):
            got = nn(gate_grad, pair[0, :, cols(c)]) + nn(up_grad, pair[1, :, cols(c)])
            got = got.reshape(count, NY, SLAB, CHUNK)
            own[k : k + count, :, cols(c)] = got[:, 0]
            part[k : k + count, :, :, cols(c)] = got[:, 1:].astype(BF16)
            return carry

        for h in range(BACK_PIECES[k]):
            over(BACK_PIECES[k], h, behind)
            for i in range(count):
                give(k + i, h)

    rl_copies = {}
    ru_copies = {}
    rd_copies = {}

    def to_upper(k, h):
        copy = remote(
            part.at[k, 0, :, piece(BACK_PIECES[k], h)],
            from_down.at[k, :, piece(BACK_PIECES[k], h)],
            rd_send.at[h, k],
            rd_recv.at[h, k],
            up,
        )
        copy.start()
        rd_copies[k, h] = copy

    def to_lower(k, h):
        copy = remote(
            part.at[k, 2, :, piece(BACK_PIECES[k], h)],
            from_up.at[k, :, piece(BACK_PIECES[k], h)],
            ru_send.at[h, k],
            ru_recv.at[h, k],
            dn,
        )
        copy.start()
        ru_copies[k, h] = copy

    def give(k, h):
        copy = remote(
            part.at[k, 1, :, piece(BACK_PIECES[k], h)],
            relayed.at[k, :, piece(BACK_PIECES[k], h)],
            rl_send.at[h, k],
            rl_recv.at[h, k],
            (up, dn)[k % 2],
        )
        copy.start()
        rl_copies[k, h] = copy
        (to_lower, to_upper)[k % 2](k, h)

    def give_on(k, h):
        rl_copies[k, h].wait_recv()
        mine = (0, 2)[k % 2]

        def add(c, carry):
            total = part[k, mine, :, cols(c)].astype(F32) + relayed[k, :, cols(c)].astype(F32)
            part[k, mine, :, cols(c)] = total.astype(BF16)
            return carry

        over(BACK_PIECES[k], h, add)
        (to_upper, to_lower)[k % 2](k, h)

    rz_copies = {}

    def settle(k, h):
        ru_copies[k, h].wait_recv()
        rd_copies[k, h].wait_recv()
        target = back if k == 0 else summed

        def add(c, carry):
            total = own[k, :, cols(c)] + (
                from_up[k, :, cols(c)].astype(F32) + from_down[k, :, cols(c)].astype(F32)
            )
            target[k, :, cols(c)] = total.astype(BF16)
            return carry

        over(BACK_PIECES[k], h, add)
        if k:
            copy = remote(
                summed.at[k, :, piece(BACK_PIECES[k], h)],
                back.at[k, :, piece(BACK_PIECES[k], h)],
                rz_send.at[h, k],
                rz_recv.at[h, k],
                at_z(NZ - OFFSETS[k]),
            )
            copy.start()
            rz_copies[k, h] = copy

    def grads(which):
        def one(c, carry):
            kind = 0 if which < 2 else 1
            data = rows[:, kind, :, :, cols(c)].reshape(NZ * per_slab, CHUNK)
            got = tn((gate_t, up_t, hid_t)[which][...], data).astype(BF16)
            if which < 2:
                gpair[which, :, cols(c)] = got
            else:
                gdown[:, cols(c)] = got
            return carry

        lax.fori_loop(0, chunks, one, 0)
    half = NXC * NZL * CAP
    qrow = lax.broadcasted_iota(jnp.int32, (half, half), 0)
    qcol = lax.broadcasted_iota(jnp.int32, (half, half), 1)
    q_src = lax.div(qrow, NZL * CAP)
    q_off = lax.rem(lax.div(qrow, CAP), NZL)
    wanted_back = q_off * SLAB + q_src * CAP + lax.rem(qrow, CAP)
    shuffle_back = jnp.where(qcol == wanted_back, 1.0, 0.0).astype(BF16)

    def add_halves(c, carry):
        parts = []
        for i in range(NZL):
            first, second = OFFSETS.index(i), OFFSETS.index(i + NZL)
            total = back[first, :, cols(c)].astype(F32) + back[second, :, cols(c)].astype(F32)
            parts.append(total.astype(BF16))
        moved = nn(shuffle_back, jnp.concatenate(parts, axis=0))
        for i in range(NXC):
            xsend[i, :, cols(c)] = moved[i * NZL * CAP : (i + 1) * NZL * CAP].astype(BF16)
        return carry

    rx_copies = []
    own_back = []

    def join(h):
        for k in range(1, NZ):
            for q in range(BACK_PIECES[k]):
                if q * END_PIECES < (h + 1) * BACK_PIECES[k] and (q + 1) * END_PIECES > h * BACK_PIECES[k]:
                    if (k, q) not in taken:
                        rz_copies[k, q].wait_recv()
                        taken.add((k, q))
        over(END_PIECES, h, add_halves)
        for i in range(1, NXC):
            copy = remote(
                xsend.at[i, :, piece(END_PIECES, h)],
                final.at[xc, :, piece(END_PIECES, h)],
                rx_send.at[h, i],
                rx_recv.at[h, i],
                at_x(NXC - i),
            )
            copy.start()
            rx_copies.append(copy)
        copy = pltpu.make_async_copy(
            xsend.at[0, :, piece(END_PIECES, h)], final.at[xc, :, piece(END_PIECES, h)], store_sem.at[h]
        )
        copy.start()
        own_back.append(copy)

    taken = set()
    loads[2].wait()
    loads[3].wait()
    steps = {
        "cross": cross,
        "spread": spread,
        "forward": forward,
        "relay": relay,
        "compute": compute,
        "give_on": give_on,
        "settle": settle,
        "grads": grads,
        "join": join,
    }
    for name, *where in ORDER:
        steps[name](*where)

    for table in (x_copies, z_copies, y_copies, f_copies, rl_copies, ru_copies, rd_copies, rz_copies):
        for copy in table.values():
            copy.wait_send()
    for copy in rx_copies:
        copy.wait()
    for copy in own_back:
        copy.wait()


def per_device(activations, cotangent, expert_ids, gate_probs, gate_up, down_proj):
    tokens, width = activations.shape
    units = down_proj.shape[1]
    pair = jnp.swapaxes(gate_up[0], 1, 2)
    down = down_proj[0]
    dma = pltpu.SemaphoreType.DMA
    vmem = pltpu.VMEM
    any_space = pl.BlockSpec(memory_space=pl.ANY)
    in_hbm = pl.BlockSpec(memory_space=pltpu.HBM)
    in_vmem = pl.BlockSpec(memory_space=pltpu.VMEM)
    total_rows = NZ * NY * SLAB
    pick, final, gpair, gdown = pl.pallas_call(
        kernel,
        out_shape=(
            jax.ShapeDtypeStruct((NXC * NZL * CAP, tokens), BF16),
            jax.ShapeDtypeStruct((NXC, NZL * CAP, width), BF16),
            pltpu.VMEM((2, units, width), BF16),
            pltpu.VMEM((units, width), BF16),
        ),
        in_specs=[in_hbm, in_hbm, in_hbm, in_hbm, in_hbm, in_hbm],
        out_specs=(in_vmem, any_space, in_vmem, in_vmem),
        scratch_shapes=[
            vmem((1, tokens), jnp.int32),
            vmem((1, tokens), F32),
            vmem((tokens, width), BF16),
            vmem((tokens, width), BF16),
            vmem((2, units, width), BF16),
            vmem((units, width), BF16),
            vmem((NXC, 2 * NZL * CAP, width), BF16),
            vmem((NXC, 2 * NZL * CAP, width), BF16),
            vmem((NZL, 2, SLAB, width), BF16),
            vmem((NZ, 2, NY, SLAB, width), BF16),
            vmem((3, 2 * NY * SLAB, units), F32),
            vmem((total_rows, units), BF16),
            vmem((total_rows, units), BF16),
            vmem((total_rows, units), BF16),
            vmem((NZ, SLAB, width), F32),
            vmem((NZ, NY - 1, SLAB, width), BF16),
            vmem((NZ, SLAB, width), BF16),
            vmem((NZ, SLAB, width), BF16),
            vmem((NZ, SLAB, width), BF16),
            vmem((NZ, SLAB, width), BF16),
            vmem((NZ, SLAB, width), BF16),
            vmem((NXC, NZL * CAP, width), BF16),
            dma((7,)),
            dma((5,)),
            dma((X_PIECES, NXC)),
            dma((X_PIECES, NXC)),
            dma((MOST, NZ)),
            dma((MOST, NZ)),
            dma((2, MOST, NZ)),
            dma((2, MOST, NZ)),
            dma((MOST, NZ)),
            dma((MOST, NZ)),
            dma((MOST, NZ)),
            dma((MOST, NZ)),
            dma((MOST, NZ)),
            dma((MOST, NZ)),
            dma((MOST, NZ)),
            dma((MOST, NZ)),
            dma((MOST, NZ)),
            dma((MOST, NZ)),
            dma((END_PIECES, NXC)),
            dma((END_PIECES, NXC)),
        ],
        compiler_params=pltpu.CompilerParams(
            collective_id=0, has_side_effects=True, vmem_limit_bytes=48 * 1024 * 1024
        ),
    )(expert_ids.reshape(1, tokens), gate_probs.reshape(1, tokens), activations, cotangent, pair, down)
    out = tn(pick, final.reshape(NXC * NZL * CAP, width)).astype(BF16)
    return out, jnp.swapaxes(gpair, 1, 2)[None], gdown[None]


def solution(mesh):
    in_specs = (
        P(("dp", "expert"), None),
        P(("dp", "expert"), None),
        P(("dp", "expert"), None),
        P(("dp", "expert"), None),
        P("expert", None, None, "dp"),
        P("expert", "dp", None),
    )
    out_specs = (P(("dp", "expert"), None), P("expert", None, None, "dp"), P("expert", "dp", None))
    return jax.shard_map(
        per_device, mesh=mesh, in_specs=in_specs, out_specs=out_specs, check_vma=False
    )
```
